128 devices in a mesh: seq: 64 (over y, x_hi, z, core), head: 2 (over x_lo).
Axes of the slice: x: 4 (x_hi: 2, x_lo: 2; x = x_hi * 2 + x_lo), y: 4, z: 4, core: 2. Of those that a mesh axis runs over, the one named last changes fastest.
Arguments:
- features: bfloat16 [65536, 1024], P('seq', 'head'), may hold values from -4.1875 to 4.1875
- cells: int32 [65536], P('seq'), may hold values from 0 to 65535, as said below
- conv7: bfloat16 [7, 7, 1024], P(None, None, 'head'), may hold values from -0.875 to 0.875
- conv5: bfloat16 [5, 5, 1024], P(None, None, 'head'), may hold values from -1.25 to 1.25
- conv3: bfloat16 [3, 3, 1024], P(None, None, 'head'), may hold values from -2 to 2
- conv_bias: bfloat16 [1024], P('head'), may hold values from -3 to 3
- w_qkv: bfloat16 [1024, 3, 1024], P(None, None, 'head'), may hold values from -5 to 5
Outputs:
- attended: bfloat16 [65536, 1024], P('seq', 'head')
The draws below stay inside these ranges and needn't reach their ends.
Inputs may be any that keep to these rules, and one draw needn't show every extreme that they name: cells names each of the 65536 grid cells once. Of the 1024 entries held by one index of seq, at most 32 lie in any one band of 1024 consecutive cells, and exactly 32 lie in some band; every band receives exactly 32 from some index of seq.
All inputs are finite; a program needn't handle non-finite values.
Results may differ from the reference program's by a relative error of at most 0.0052.
Values may be sent and summed in bfloat16 or wider, within the bound.
No kernel may reach another device: no remote copies, remote signals or barrier semaphores. Data moves between devices by JAX's collectives and lax.ppermute only.
A program may use at most 128 MiB of HBM per device.

```python
import math
import jax
import jax.numpy as jnp
from jax import lax

D = 1024
HEADS = 16
HEAD_DIM = 64
GRID_W = 256
TOK_DEV = 1024
ROWS = 256
TOKENS = 65536
N_SEQ = 64


def draw_cells(key, part):
    members = TOKENS // TOK_DEV
    half_load = TOK_DEV // members
    first, second, third, fourth = jax.random.split(key, 4)
    spread = jax.random.randint(first, (members // 2,), 0, half_load + 1).astype(jnp.int32)
    spread = spread.at[0].set(half_load)
    shift_loads = jnp.stack([half_load + spread, half_load - spread], axis=1).reshape(members)
    shift_order = jax.random.permutation(second, members)
    shift_loads = shift_loads[shift_order]
    seg_ends = jnp.cumsum(shift_loads)
    slot_index = jnp.arange(TOK_DEV, dtype=jnp.int32)
    shift_of = jnp.sum((seg_ends[None, :] <= slot_index[:, None]).astype(jnp.int32), axis=1)
    band_perms = jax.vmap(lambda sub_key: jax.random.permutation(sub_key, TOK_DEV))(jax.random.split(third, members)).astype(jnp.int32)
    source = jnp.arange(members, dtype=jnp.int32)
    band_of = (source[:, None] - shift_of[None, :] + members) % members
    cell_ids = band_of * TOK_DEV + band_perms[band_of, slot_index[None, :]]
    scramble = jax.vmap(lambda sub_key: jax.random.permutation(sub_key, TOK_DEV))(jax.random.split(fourth, members)).astype(jnp.int32)
    cell_ids = jnp.take_along_axis(cell_ids, scramble, axis=1)
    return cell_ids.reshape(TOKENS).astype(jnp.int32)


def draw_w_qkv(key, part):
    noise = jax.random.normal(key, (D, 3, D), jnp.float32) * (1.0 / math.sqrt(D))
    return noise.astype(jnp.bfloat16)


def block_levels(stream_key, extent, shards, low, high):
    gain = 1.0
    for position, parts in shards:
        draws = jax.random.uniform(jax.random.fold_in(jax.random.fold_in(stream_key, 6), position), (parts,), jnp.float32, low / len(shards), high / len(shards))
        gain = gain * jnp.repeat(jnp.exp(draws), extent[position] // parts).reshape((-1,) + (1,) * (len(extent) - 1 - position))
    return gain


def gaussian(rng, shape, scale, limit, shards=(), held_as=jnp.bfloat16):
    values = jax.random.normal(rng, shape, jnp.float32) * scale
    if len(shards) > 0:
        values = block_levels(rng, shape, shards, -0.22, 0.18) * values
    return jnp.clip(values, min=-limit, max=limit).astype(held_as)


def setup_inputs(seed: int = 0) -> dict:
    streams_of = jax.random.split(jax.random.key(seed), 8)
    features = gaussian(streams_of[0], (TOKENS, D), 0.7, 4.1875, ((0, 64), (1, 2)))
    cells = draw_cells(jax.random.fold_in(streams_of[7], 71), 0)
    conv7 = gaussian(streams_of[2], (7, 7, D), 49 ** -0.5, 0.875, ((2, 2),))
    conv5 = gaussian(streams_of[3], (5, 5, D), 25 ** -0.5, 1.25, ((2, 2),))
    conv3 = gaussian(streams_of[4], (3, 3, D), 9 ** -0.5, 2.0, ((2, 2),))
    conv_bias = gaussian(streams_of[5], (D,), 0.5, 3.0, ((0, 2),))
    w_qkv = draw_w_qkv(jax.random.fold_in(streams_of[7], 71), 0)
    return {"features": features, "cells": cells, "conv7": conv7, "conv5": conv5, "conv3": conv3, "conv_bias": conv_bias, "w_qkv": w_qkv}


def depthwise(padded, kernel, margin, height, width):
    reach = kernel.shape[0]
    result = jnp.zeros((height, width, padded.shape[2]), jnp.float32)
    for i in range(reach):
        for j in range(reach):
            result = result + padded[margin + i:margin + i + height, margin + j:margin + j + width] * kernel[i, j].astype(jnp.float32)
    return result

def reference(features, cells, conv7, conv5, conv3, conv_bias, w_qkv):
    placed = jnp.zeros((TOKENS, D), jnp.bfloat16).at[cells].set(features)
    grid_cells = placed.reshape(ROWS, GRID_W, D).astype(jnp.float32)
    padded = jnp.pad(grid_cells, ((3, 3), (3, 3), (0, 0)))
    mixed_sum = grid_cells + conv_bias.astype(jnp.float32)
    for kernel in (conv7, conv5, conv3):
        mixed_sum = mixed_sum + depthwise(padded, kernel, 3 - kernel.shape[0] // 2, ROWS, GRID_W)
    ppeg = mixed_sum.astype(jnp.bfloat16).reshape(TOKENS, D)
    projected = jnp.dot(ppeg, w_qkv.reshape(D, 3 * D), preferred_element_type=jnp.float32).astype(jnp.bfloat16)
    queries = projected[:, :D].reshape(TOKENS, HEADS, HEAD_DIM)
    key_rows = projected[:, D:2 * D].reshape(TOKENS, HEADS, HEAD_DIM)
    value_rows = projected[:, 2 * D:].reshape(TOKENS, HEADS, HEAD_DIM)
    score_scale = 1.0 / math.sqrt(HEAD_DIM)

    def attend(band_index):
        start = (band_index * TOK_DEV).astype(jnp.int32)
        before = ((band_index + N_SEQ - 1) % N_SEQ * TOK_DEV).astype(jnp.int32)
        query_band = lax.dynamic_slice_in_dim(queries, start, TOK_DEV, 0).astype(jnp.float32)
        key_band = jnp.concatenate([lax.dynamic_slice_in_dim(key_rows, start, TOK_DEV, 0), lax.dynamic_slice_in_dim(key_rows, before, TOK_DEV, 0)], axis=0).astype(jnp.float32)
        value_band = jnp.concatenate([lax.dynamic_slice_in_dim(value_rows, start, TOK_DEV, 0), lax.dynamic_slice_in_dim(value_rows, before, TOK_DEV, 0)], axis=0).astype(jnp.float32)
        scores = jnp.einsum('thd,uhd->thu', query_band, key_band) * score_scale
        row_top = lax.optimization_barrier(jnp.max(scores, axis=2, keepdims=True))
        weight = jnp.exp(scores - row_top)
        weight_sum = lax.optimization_barrier(jnp.sum(weight, axis=2))
        probs = lax.optimization_barrier(weight.astype(jnp.bfloat16)).astype(jnp.float32)
        summed = jnp.einsum('thu,uhd->thd', probs, value_band)
        return (summed / weight_sum[:, :, None]).astype(jnp.bfloat16).reshape(TOK_DEV, D)
    attended = lax.map(attend, jnp.arange(N_SEQ, dtype=jnp.int32))
    return attended.reshape(TOKENS, D)
```

```python
import functools
import math

import jax
import jax.numpy as jnp
from jax import lax
from jax.experimental import pallas as pl
from jax.experimental.pallas import tpu as pltpu
from jax.sharding import PartitionSpec as P

D = 1024
HEADS = 16
GRID_W = 256
BANDS = 64
TOK = 1024
LOCAL = 512
CAP = 32
MSG = 4 * CAP + 8
BF16 = jnp.bfloat16
F32 = jnp.float32
VMEM_BYTES = 56 * 1024 * 1024


def iota(shape, dim):
    return lax.broadcasted_iota(jnp.int32, shape, dim)


def ones_where(mask):
    return jnp.where(mask, 1.0, 0.0).astype(BF16)


def params(**kwargs):
    return pltpu.CompilerParams(vmem_limit_bytes=VMEM_BYTES, **kwargs)


def pack_kernel(cells_ref, feat_ref, out_ref, slot_ref, info_ref):
    step = pl.program_id(0)

    @pl.when(step == 0)
    def _():
        cells = cells_ref[...]
        band = cells >> 10
        within = cells & (TOK - 1)
        member = jnp.where(iota((BANDS, TOK), 0) == band, 1.0, 0.0)
        before = ones_where(iota((TOK, TOK), 0) < iota((TOK, TOK), 1))
        counts = jnp.dot(member.astype(BF16), before, preferred_element_type=F32)
        rank = jnp.sum(member * counts, axis=0, keepdims=True).astype(jnp.int32)
        slot_ref[...] = band * CAP + rank
        place = (within & 768) | ((within & 31) << 3) | ((within >> 5) & 7)
        row = iota((16, TOK), 0)
        info = jnp.where(row == 0, (place >> 5) + 1, jnp.where(row == 1, place & 31, 0))
        info_ref[...] = info.astype(F32).astype(BF16)

    chosen = ones_where(slot_ref[...] - step * 256 == iota((256, TOK), 0))
    rows = jnp.dot(chosen, feat_ref[...], preferred_element_type=F32).astype(BF16)
    for c in range(4):
        out_ref[:, c * CAP : (c + 1) * CAP, :] = rows[:, c * 128 : (c + 1) * 128].reshape(8, CAP, 128)
    info = lax.dot_general(
        info_ref[...], chosen, (((1,), (1,)), ((), ())), preferred_element_type=F32
    )
    group = iota((8, 128), 1) // CAP
    for d in range(8):
        own = jnp.where(group == d % 4, info[:8, d // 4 * 128 : d // 4 * 128 + 128], 0.0)
        own = own + pltpu.roll(own, 64, 1)
        own = own + pltpu.roll(own, 32, 1)
        out_ref[d, 4 * CAP :, :] = own.astype(BF16)


def pack(cells, features):
    return pl.pallas_call(
        pack_kernel,
        grid=(8,),
        in_specs=[
            pl.BlockSpec((1, TOK), lambda i: (0, 0)),
            pl.BlockSpec((TOK, LOCAL), lambda i: (0, 0)),
        ],
        out_specs=pl.BlockSpec((8, MSG, 128), lambda i: (i, 0, 0)),
        out_shape=jax.ShapeDtypeStruct((BANDS, MSG, 128), BF16),
        scratch_shapes=[pltpu.VMEM((1, TOK), jnp.int32), pltpu.VMEM((16, TOK), BF16)],
        compiler_params=params(),
        name="pack",
    )(cells.reshape(1, TOK), features)


def place_kernel(msg_ref, out_ref, place_ref):
    step = pl.program_id(0)

    @pl.when(step == 0)
    def _():
        info = msg_ref[:, 4 * CAP :, :].astype(F32).reshape(16, 4, 8, 128)
        shape = (16, 4, 8, 128)
        info = jnp.sum(jnp.where(iota(shape, 3) // CAP == iota(shape, 1), info, 0.0), axis=1)
        place_ref[...] = (info[:, 0, :] * 32.0 + info[:, 1, :]).astype(jnp.int32) - 32

    cell = iota((256, 128), 0) + step * 256
    chosen = jnp.concatenate(
        [ones_where(place_ref[g : g + 1, :] == cell) for g in range(16)], axis=1
    )
    rows = jnp.concatenate(
        [msg_ref[:, c * CAP : (c + 1) * CAP, :].reshape(BANDS * CAP, 128) for c in range(4)],
        axis=1,
    )
    out_ref[...] = jnp.dot(chosen, rows, preferred_element_type=F32).astype(BF16)


def place(messages):
    return pl.pallas_call(
        place_kernel,
        grid=(4,),
        in_specs=[pl.BlockSpec((BANDS, MSG, 128), lambda i: (0, 0, 0))],
        out_specs=pl.BlockSpec((256, LOCAL), lambda i: (i, 0)),
        out_shape=jax.ShapeDtypeStruct((TOK, LOCAL), BF16),
        scratch_shapes=[pltpu.VMEM((16, 128), jnp.int32)],
        compiler_params=params(),
        name="place",
    )(messages)


def conv_kernel(band_ref, above_ref, below_ref, w_ref, bias_ref, out_ref, x_ref, tap_ref, nat_ref):
    sub = iota((3, 8, 128), 1)
    for r in range(10):
        if r < 3:
            rows = above_ref[r * 256 : (r + 1) * 256, :]
        elif r < 7:
            rows = band_ref[(r - 3) * 256 : (r - 2) * 256, :]
        else:
            rows = below_ref[(r - 7) * 256 : (r - 6) * 256, :]
        x = rows.astype(F32).reshape(32, 8, 128)
        x_ref[r, 3:35] = x
        x_ref[r, 0:3] = jnp.where(sub == 0, 0.0, pltpu.roll(x[29:32], 1, 1))
        x_ref[r, 35:38] = jnp.where(sub == 7, 0.0, pltpu.roll(x[0:3], 7, 1))
    for t in range(49):
        tap_ref[t] = jnp.broadcast_to(w_ref[t : t + 1, :], (8, 128))
    bias = jnp.broadcast_to(bias_ref[...], (8, 128))

    def group(g, carry):
        k = g * 4
        acc = [[bias] * 4 for _ in range(4)]
        for j in range(7):
            taps = [tap_ref[i * 7 + j] for i in range(7)]
            for r in range(10):
                for n in range(4):
                    x = x_ref[r, k + j + n]
                    for i in range(7):
                        if 0 <= r - i < 4:
                            acc[r - i][n] = acc[r - i][n] + x * taps[i]
        for o in range(4):
            for n in range(4):
                nat_ref[pl.ds(o * 256 + k + n, 8, stride=32), :] = acc[o][n]
        return carry

    lax.fori_loop(0, 8, group, 0)
    out_ref[...] = nat_ref[...].astype(BF16)


def conv(band, above, below, taps, bias):
    return pl.pallas_call(
        conv_kernel,
        grid=(4,),
        in_specs=[
            pl.BlockSpec((TOK, 128), lambda i: (0, i)),
            pl.BlockSpec((768, 128), lambda i: (0, i)),
            pl.BlockSpec((768, 128), lambda i: (0, i)),
            pl.BlockSpec((49, 128), lambda i: (0, i)),
            pl.BlockSpec((1, 128), lambda i: (0, i)),
        ],
        out_specs=pl.BlockSpec((TOK, 128), lambda i: (0, i)),
        out_shape=jax.ShapeDtypeStruct((TOK, LOCAL), BF16),
        scratch_shapes=[
            pltpu.VMEM((10, 38, 8, 128), F32),
            pltpu.VMEM((49, 8, 128), F32),
            pltpu.VMEM((TOK, 128), F32),
        ],
        compiler_params=params(),
        name="conv",
    )(band, above, below, taps, bias)


def project_kernel(half_ref, own_ref, other_ref, w_own_ref, w_other_ref, out_ref):
    out_ref[...] = (
        jnp.dot(own_ref[...], w_own_ref[...], preferred_element_type=F32)
        + jnp.dot(other_ref[...], w_other_ref[...], preferred_element_type=F32)
    ).astype(BF16)


def project(half, own, other, weights, first, width):
    rows = own.shape[0]
    return pl.pallas_call(
        project_kernel,
        grid_spec=pltpu.PrefetchScalarGridSpec(
            num_scalar_prefetch=1,
            grid=(rows // 256, width),
            in_specs=[
                pl.BlockSpec((256, LOCAL), lambda i, j, h: (i, 0)),
                pl.BlockSpec((256, LOCAL), lambda i, j, h: (i, 0)),
                pl.BlockSpec((LOCAL, LOCAL), lambda i, j, h: (h[0], first + j)),
                pl.BlockSpec((LOCAL, LOCAL), lambda i, j, h: (1 - h[0], first + j)),
            ],
            out_specs=pl.BlockSpec((256, LOCAL), lambda i, j, h: (i, j)),
        ),
        out_shape=jax.ShapeDtypeStruct((rows, width * LOCAL), BF16),
        compiler_params=params(),
        cost_estimate=pl.CostEstimate(
            flops=2 * rows * D * width * LOCAL,
            bytes_accessed=2 * (rows * D + (rows + D) * width * LOCAL),
            transcendentals=0,
        ),
        name="project",
    )(half, own, other, weights, weights)


def partial_attention(q_ref, k_ref, v_ref):
    q, k = q_ref[...], k_ref[...]
    lane = iota(q.shape, 1)
    v = jnp.concatenate([v_ref[...], jnp.ones(v_ref.shape, BF16)], axis=1)
    parts = []
    for head in range(2):
        mine = (lane // 64) == head
        scores = lax.dot_general(
            jnp.where(mine, q * 0.125, 0.0).astype(BF16),
            k,
            (((1,), (1,)), ((), ())),
            preferred_element_type=F32,
        )
        top = jnp.max(scores, axis=1, keepdims=True)
        weight = jnp.exp(scores - top).astype(BF16)
        summed = jnp.dot(weight, v, preferred_element_type=F32)
        parts.append((summed[:, :128], summed[:, 128:], jnp.broadcast_to(top, q.shape)))
    first = lane < 64
    return [jnp.where(first, a, b) for a, b in zip(*parts)]


def own_kernel(q_ref, k_ref, v_ref, acc_ref, sum_ref, top_ref):
    acc_ref[...], sum_ref[...], top_ref[...] = partial_attention(q_ref, k_ref, v_ref)


def prior_kernel(q_ref, k_ref, v_ref, acc_ref, sum_ref, top_ref, out_ref):
    acc, total, top = partial_attention(q_ref, k_ref, v_ref)
    highest = jnp.maximum(top, top_ref[...])
    here, there = jnp.exp(top - highest), jnp.exp(top_ref[...] - highest)
    total = total * here + sum_ref[...] * there
    out_ref[...] = ((acc * here + acc_ref[...] * there) / total).astype(BF16)


QROWS = 256


def attend(queries, keys_values, state=None):
    block = pl.BlockSpec((QROWS, 128), lambda p, i: (i, p))
    in_specs = [
        block,
        pl.BlockSpec((TOK, 128), lambda p, i: (0, p)),
        pl.BlockSpec((TOK, 128), lambda p, i: (0, 4 + p)),
    ]
    cost = pl.CostEstimate(
        flops=4 * TOK * TOK * LOCAL, bytes_accessed=10 * 2**20, transcendentals=8 * TOK * TOK
    )
    if state is None:
        return pl.pallas_call(
            own_kernel,
            grid=(4, TOK // QROWS),
            in_specs=in_specs,
            out_specs=[block] * 3,
            out_shape=[jax.ShapeDtypeStruct((TOK, LOCAL), F32)] * 3,
            compiler_params=params(),
            cost_estimate=cost,
            name="own_keys",
        )(queries, keys_values, keys_values)
    return pl.pallas_call(
        prior_kernel,
        grid=(4, TOK // QROWS),
        in_specs=in_specs + [block] * 3,
        out_specs=block,
        out_shape=jax.ShapeDtypeStruct((TOK, LOCAL), BF16),
        compiler_params=params(),
        cost_estimate=cost,
        name="prior_keys",
    )(queries, keys_values, keys_values, *state)


def merged_taps(conv7, conv5, conv3):
    taps = conv7.astype(F32)
    taps = taps + jnp.pad(conv5.astype(F32), ((1, 1), (1, 1), (0, 0)))
    taps = taps + jnp.pad(conv3.astype(F32), ((2, 2), (2, 2), (0, 0)))
    return taps.reshape(49, LOCAL) + (jnp.arange(49) == 24).astype(F32)[:, None]


def shards(features, cells, conv7, conv5, conv3, conv_bias, w_qkv):
    messages = pack(cells, features)
    arrived = lax.all_to_all(messages, "seq", split_axis=0, concat_axis=0, tiled=True)
    band = place(arrived)
    up = [(i, i + 1) for i in range(BANDS - 1)]
    down = [(j, i) for i, j in up]
    above = lax.ppermute(band[256:], "seq", up)
    below = lax.ppermute(band[:768], "seq", down)
    taps = merged_taps(conv7, conv5, conv3)
    ppeg = conv(band, above, below, taps, conv_bias.astype(F32).reshape(1, LOCAL))
    other = lax.ppermute(ppeg, "head", [(0, 1), (1, 0)])
    weights = w_qkv.reshape(D, 3 * LOCAL)
    half = lax.axis_index("head").astype(jnp.int32).reshape(1)
    keys_values = project(half, ppeg, other, weights, 1, 2)
    prior = lax.ppermute(keys_values, "seq", [(i, (i + 1) % BANDS) for i in range(BANDS)])
    queries = project(half, ppeg, other, weights, 0, 1)
    state = attend(queries, keys_values)
    return attend(queries, prior, state)


def solution(mesh):
    placed = (
        P("seq", "head"),
        P("seq"),
        P(None, None, "head"),
        P(None, None, "head"),
        P(None, None, "head"),
        P("head"),
        P(None, None, "head"),
    )
    return jax.shard_map(
        shards, mesh=mesh, in_specs=placed, out_specs=P("seq", "head"), check_vma=False
    )
```

```python
import functools
import math

import jax
import jax.numpy as jnp
from jax import lax
from jax.experimental import pallas as pl
from jax.experimental.pallas import tpu as pltpu
from jax.sharding import PartitionSpec as P

D = 1024
HEADS = 16
GRID_W = 256
BANDS = 64
TOK = 1024
LOCAL = 512
CAP = 32
MSG = 4 * CAP + 8
BF16 = jnp.bfloat16
F32 = jnp.float32
VMEM_BYTES = 56 * 1024 * 1024


def iota(shape, dim):
    return lax.broadcasted_iota(jnp.int32, shape, dim)


def ones_where(mask):
    return jnp.where(mask, 1.0, 0.0).astype(BF16)


def params(**kwargs):
    return pltpu.CompilerParams(vmem_limit_bytes=VMEM_BYTES, **kwargs)


def pack_kernel(cells_ref, feat_ref, out_ref, slot_ref, info_ref):
    step = pl.program_id(0)

    @pl.when(step == 0)
    def _():
        cells = cells_ref[...]
        band = cells >> 10
        within = cells & (TOK - 1)
        member = jnp.where(iota((BANDS, TOK), 0) == band, 1.0, 0.0)
        before = ones_where(iota((TOK, TOK), 0) < iota((TOK, TOK), 1))
        counts = jnp.dot(member.astype(BF16), before, preferred_element_type=F32)
        rank = jnp.sum(member * counts, axis=0, keepdims=True).astype(jnp.int32)
        slot_ref[...] = band * CAP + rank
        place = (within & 768) | ((within & 31) << 3) | ((within >> 5) & 7)
        row = iota((16, TOK), 0)
        info = jnp.where(row == 0, (place >> 5) + 1, jnp.where(row == 1, place & 31, 0))
        info_ref[...] = info.astype(F32).astype(BF16)

    chosen = ones_where(slot_ref[...] - step * 256 == iota((256, TOK), 0))
    rows = jnp.dot(chosen, feat_ref[...], preferred_element_type=F32).astype(BF16)
    for c in range(4):
        out_ref[:, c * CAP : (c + 1) * CAP, :] = rows[:, c * 128 : (c + 1) * 128].reshape(8, CAP, 128)
    info = lax.dot_general(
        info_ref[...], chosen, (((1,), (1,)), ((), ())), preferred_element_type=F32
    )
    group = iota((8, 128), 1) // CAP
    for d in range(8):
        own = jnp.where(group == d % 4, info[:8, d // 4 * 128 : d // 4 * 128 + 128], 0.0)
        own = own + pltpu.roll(own, 64, 1)
        own = own + pltpu.roll(own, 32, 1)
        out_ref[d, 4 * CAP :, :] = own.astype(BF16)


def pack(cells, features):
    return pl.pallas_call(
        pack_kernel,
        grid=(8,),
        in_specs=[
            pl.BlockSpec((1, TOK), lambda i: (0, 0)),
            pl.BlockSpec((TOK, LOCAL), lambda i: (0, 0)),
        ],
        out_specs=pl.BlockSpec((8, MSG, 128), lambda i: (i, 0, 0)),
        out_shape=jax.ShapeDtypeStruct((BANDS, MSG, 128), BF16),
        scratch_shapes=[pltpu.VMEM((1, TOK), jnp.int32), pltpu.VMEM((16, TOK), BF16)],
        compiler_params=params(),
        name="pack",
    )(cells.reshape(1, TOK), features)


def place_kernel(msg_ref, first_ref, last_ref, place_ref):
    step = pl.program_id(0)

    @pl.when(step == 0)
    def _():
        info = msg_ref[:, 4 * CAP :, :].astype(F32).reshape(16, 4, 8, 128)
        shape = (16, 4, 8, 128)
        info = jnp.sum(jnp.where(iota(shape, 3) // CAP == iota(shape, 1), info, 0.0), axis=1)
        place_ref[...] = (info[:, 0, :] * 32.0 + info[:, 1, :]).astype(jnp.int32) - 32

    cell = iota((256, 128), 0) + step * 256
    chosen = jnp.concatenate(
        [ones_where(place_ref[g : g + 1, :] == cell) for g in range(16)], axis=1
    )
    rows = jnp.concatenate(
        [msg_ref[:, c * CAP : (c + 1) * CAP, :].reshape(BANDS * CAP, 128) for c in range(4)],
        axis=1,
    )
    row = jnp.dot(chosen, rows, preferred_element_type=F32).astype(BF16)

    @pl.when(step < 3)
    def _():
        first_ref[...] = row

    @pl.when(step > 0)
    def _():
        last_ref[...] = row


def place(messages):
    return pl.pallas_call(
        place_kernel,
        grid=(4,),
        in_specs=[pl.BlockSpec((BANDS, MSG, 128), lambda i: (0, 0, 0))],
        out_specs=[
            pl.BlockSpec((256, LOCAL), lambda i: (jnp.minimum(i, 2), 0)),
            pl.BlockSpec((256, LOCAL), lambda i: (jnp.maximum(i - 1, 0), 0)),
        ],
        out_shape=[jax.ShapeDtypeStruct((768, LOCAL), BF16)] * 2,
        scratch_shapes=[pltpu.VMEM((16, 128), jnp.int32)],
        compiler_params=params(),
        name="place",
    )(messages)


def conv_kernel(far_ref, first_ref, last_ref, near_ref, w_ref, bias_ref, out_ref, x_ref, tap_ref, nat_ref, *, upper):
    sub = iota((3, 8, 128), 1)
    own = [(first_ref, 0), (first_ref, 1), (first_ref, 2), (last_ref, 2)]
    far = [(far_ref, r) for r in range(3)]
    sources = far + own + [(near_ref, 0)] if upper else [(near_ref, 0)] + own + far
    for r, (ref, at) in enumerate(sources):
        x = ref[at * 256 : (at + 1) * 256, :].astype(F32).reshape(32, 8, 128)
        x_ref[r, 3:35] = x
        x_ref[r, 0:3] = jnp.where(sub == 0, 0.0, pltpu.roll(x[29:32], 1, 1))
        x_ref[r, 35:38] = jnp.where(sub == 7, 0.0, pltpu.roll(x[0:3], 7, 1))
    for t in range(49):
        tap_ref[t] = jnp.broadcast_to(w_ref[t : t + 1, :], (8, 128))
    bias = jnp.broadcast_to(bias_ref[...], (8, 128))

    def group(g, carry):
        k = g * KGROUP
        acc = [[bias] * KGROUP for _ in range(2)]
        for j in range(7):
            for r in range(8):
                taps = [tap_ref[(r - o) * 7 + j] if 0 <= r - o < 7 else None for o in range(2)]
                for n in range(KGROUP):
                    x = x_ref[r, k + j + n]
                    for o in range(2):
                        if taps[o] is not None:
                            acc[o][n] = acc[o][n] + x * taps[o]
        for o in range(2):
            for n in range(KGROUP):
                nat_ref[pl.ds(o * 256 + k + n, 8, stride=32), :] = acc[o][n]
        return carry

    lax.fori_loop(0, 32 // KGROUP, group, 0)
    out_ref[...] = nat_ref[...].astype(BF16)


KGROUP = 8


def conv(first, last, above, below, taps, bias, upper):
    column = lambda rows, at=0: pl.BlockSpec((rows, 128), lambda i: (at, i))
    far, near = (above, below) if upper else (below, above)
    return pl.pallas_call(
        functools.partial(conv_kernel, upper=upper),
        grid=(4,),
        in_specs=[
            column(768), column(768), column(768), column(256, 0 if upper else 2), column(49), column(1),
        ],
        out_specs=column(512),
        out_shape=jax.ShapeDtypeStruct((512, LOCAL), BF16),
        scratch_shapes=[
            pltpu.VMEM((8, 38, 8, 128), F32),
            pltpu.VMEM((49, 8, 128), F32),
            pltpu.VMEM((512, 128), F32),
        ],
        compiler_params=params(),
        cost_estimate=pl.CostEstimate(flops=98 * 512 * LOCAL, bytes_accessed=4 * 2**20, transcendentals=0),
        name="conv_upper" if upper else "conv_lower",
    )(far, first, last, near, taps, bias)


def project_kernel(half_ref, own_ref, other_ref, w_own_ref, w_other_ref, kv_ref, q_ref):
    step = pl.program_id(0)
    out = (
        jnp.dot(own_ref[...], w_own_ref[...], preferred_element_type=F32)
        + jnp.dot(other_ref[...], w_other_ref[...], preferred_element_type=F32)
    ).astype(BF16)

    @pl.when(step < 2)
    def _():
        kv_ref[...] = out

    @pl.when(step == 2)
    def _():
        q_ref[...] = out


def project(half, own, other, weights):
    rows = own.shape[0]
    third = lambda j: jnp.where(j == 2, 0, j + 1)
    return pl.pallas_call(
        project_kernel,
        grid_spec=pltpu.PrefetchScalarGridSpec(
            num_scalar_prefetch=1,
            grid=(3,),
            in_specs=[
                pl.BlockSpec((rows, LOCAL), lambda j, h: (0, 0)),
                pl.BlockSpec((rows, LOCAL), lambda j, h: (0, 0)),
                pl.BlockSpec((LOCAL, LOCAL), lambda j, h: (h[0], third(j))),
                pl.BlockSpec((LOCAL, LOCAL), lambda j, h: (1 - h[0], third(j))),
            ],
            out_specs=[
                pl.BlockSpec((rows, LOCAL), lambda j, h: (0, jnp.minimum(j, 1))),
                pl.BlockSpec((rows, LOCAL), lambda j, h: (0, 0)),
            ],
        ),
        out_shape=[
            jax.ShapeDtypeStruct((rows, 2 * LOCAL), BF16),
            jax.ShapeDtypeStruct((rows, LOCAL), BF16),
        ],
        compiler_params=params(),
        cost_estimate=pl.CostEstimate(
            flops=2 * rows * D * 3 * LOCAL, bytes_accessed=6 * 2**20, transcendentals=0
        ),
        name="project",
    )(half, own, other, weights, weights)


def partial_attention(queries, keys, values):
    v = jnp.concatenate([values, jnp.ones(values.shape, BF16)], axis=1)
    lane = iota(queries[0].shape, 1)

    def scores(step):
        mine = (lane // 64) == step % 2
        return lax.dot_general(
            jnp.where(mine, queries[step // 2] * 0.125, 0.0).astype(BF16),
            keys,
            (((1,), (1,)), ((), ())),
            preferred_element_type=F32,
        )

    ready, parts = scores(0), []
    for step in range(2 * len(queries)):
        current = ready
        if step + 1 < 2 * len(queries):
            ready = scores(step + 1)
        top = jnp.max(current, axis=1, keepdims=True)
        weight = jnp.exp(current - top).astype(BF16)
        summed = jnp.dot(weight, v, preferred_element_type=F32)
        parts.append((summed[:, :128], summed[:, 128:], jnp.broadcast_to(top, lane.shape)))
        if step % 2:
            yield [jnp.where(lane < 64, a, b) for a, b in zip(*parts)]
            parts = []


QROWS = 256


def blocks_of(*refs):
    return [
        (ref[r : r + QROWS, :]) for ref in refs for r in range(0, ref.shape[0], QROWS)
    ]


def stacked(*refs):
    return jnp.concatenate([ref[...] for ref in refs], axis=0)


def own_kernel(q0_ref, q1_ref, k0_ref, k1_ref, v0_ref, v1_ref, acc_ref, sum_ref, top_ref):
    parts = partial_attention(
        blocks_of(q0_ref, q1_ref), stacked(k0_ref, k1_ref), stacked(v0_ref, v1_ref)
    )
    for i, (acc, total, top) in enumerate(parts):
        rows = slice(i * QROWS, (i + 1) * QROWS)
        acc_ref[rows, :], sum_ref[rows, :], top_ref[rows, :] = acc, total, top


def prior_kernel(
    q0_ref, q1_ref, k0_ref, k1_ref, v0_ref, v1_ref, acc_ref, sum_ref, top_ref, out_ref
):
    parts = partial_attention(
        blocks_of(q0_ref, q1_ref), stacked(k0_ref, k1_ref), stacked(v0_ref, v1_ref)
    )
    for i, (acc, total, top) in enumerate(parts):
        rows = slice(i * QROWS, (i + 1) * QROWS)
        highest = jnp.maximum(top, top_ref[rows, :])
        here, there = jnp.exp(top - highest), jnp.exp(top_ref[rows, :] - highest)
        total = total * here + sum_ref[rows, :] * there
        out_ref[rows, :] = ((acc * here + acc_ref[rows, :] * there) / total).astype(BF16)


def attend(queries, keys_values, state=None):
    column = lambda rows, first=0: pl.BlockSpec((rows, 128), lambda p: (0, first + p))
    in_specs = [column(512)] * 4 + [column(512, 4)] * 2
    cost = pl.CostEstimate(
        flops=4 * TOK * TOK * LOCAL, bytes_accessed=10 * 2**20, transcendentals=8 * TOK * TOK
    )
    if state is None:
        return pl.pallas_call(
            own_kernel,
            grid=(4,),
            in_specs=in_specs,
            out_specs=[column(TOK)] * 3,
            out_shape=[jax.ShapeDtypeStruct((TOK, LOCAL), F32)] * 3,
            compiler_params=params(),
            cost_estimate=cost,
            name="own_keys",
        )(*queries, *keys_values, *keys_values)
    return pl.pallas_call(
        prior_kernel,
        grid=(4,),
        in_specs=in_specs + [column(TOK)] * 3,
        out_specs=column(TOK),
        out_shape=jax.ShapeDtypeStruct((TOK, LOCAL), BF16),
        compiler_params=params(),
        cost_estimate=cost,
        name="prior_keys",
    )(*queries, *keys_values, *keys_values, *state)


def merged_taps(conv7, conv5, conv3):
    taps = conv7.astype(F32)
    taps = taps + jnp.pad(conv5.astype(F32), ((1, 1), (1, 1), (0, 0)))
    taps = taps + jnp.pad(conv3.astype(F32), ((2, 2), (2, 2), (0, 0)))
    return taps.reshape(49, LOCAL) + (jnp.arange(49) == 24).astype(F32)[:, None]


def shards(features, cells, conv7, conv5, conv3, conv_bias, w_qkv):
    messages = pack(cells, features)
    arrived = lax.all_to_all(messages, "seq", split_axis=0, concat_axis=0, tiled=True)
    first, last = place(arrived)
    up = [(i, i + 1) for i in range(BANDS - 1)]
    down = [(j, i) for i, j in up]
    above = lax.ppermute(last, "seq", up)
    below = lax.ppermute(first, "seq", down)
    taps = merged_taps(conv7, conv5, conv3)
    bias = conv_bias.astype(F32).reshape(1, LOCAL)
    weights = w_qkv.reshape(D, 3 * LOCAL)
    half = lax.axis_index("head").astype(jnp.int32).reshape(1)
    ring = [(i, (i + 1) % BANDS) for i in range(BANDS)]
    mixed = [conv(first, last, above, below, taps, bias, upper) for upper in (True, False)]
    others = [lax.ppermute(own, "head", [(0, 1), (1, 0)]) for own in mixed]
    keys_values, queries = zip(
        *[project(half, own, other, weights) for own, other in zip(mixed, others)]
    )
    prior = [lax.ppermute(block, "seq", ring) for block in keys_values]
    state = attend(queries, keys_values)
    return attend(queries, prior, state)


def solution(mesh):
    placed = (
        P("seq", "head"),
        P("seq"),
        P(None, None, "head"),
        P(None, None, "head"),
        P(None, None, "head"),
        P("head"),
        P(None, None, "head"),
    )
    return jax.shard_map(
        shards, mesh=mesh, in_specs=placed, out_specs=P("seq", "head"), check_vma=False
    )
```

```python
import functools
import math

import jax
import jax.numpy as jnp
from jax import lax
from jax.experimental import pallas as pl
from jax.experimental.pallas import tpu as pltpu
from jax.sharding import PartitionSpec as P

D = 1024
HEADS = 16
GRID_W = 256
BANDS = 64
TOK = 1024
LOCAL = 512
CAP = 32
MSG = 4 * CAP + 8
BF16 = jnp.bfloat16
F32 = jnp.float32


def iota(shape, dim):
    return lax.broadcasted_iota(jnp.int32, shape, dim)


def ones_where(mask):
    return jnp.where(mask, 1.0, 0.0).astype(BF16)


def params(mebibytes):
    return pltpu.CompilerParams(vmem_limit_bytes=mebibytes * 2**20)


def pack_kernel(cells_ref, feat_ref, out_ref, slot_ref, info_ref):
    step = pl.program_id(0)

    @pl.when(step == 0)
    def _():
        cells = cells_ref[...]
        band = cells >> 10
        within = cells & (TOK - 1)
        member = jnp.where(iota((BANDS, TOK), 0) == band, 1.0, 0.0)
        before = ones_where(iota((TOK, TOK), 0) < iota((TOK, TOK), 1))
        counts = jnp.dot(member.astype(BF16), before, preferred_element_type=F32)
        rank = jnp.sum(member * counts, axis=0, keepdims=True).astype(jnp.int32)
        slot_ref[...] = band * CAP + rank
        place = (within & 768) | ((within & 31) << 3) | ((within >> 5) & 7)
        row = iota((16, TOK), 0)
        info = jnp.where(row == 0, (place >> 5) + 1, jnp.where(row == 1, place & 31, 0))
        info_ref[...] = info.astype(F32).astype(BF16)

    chosen = ones_where(slot_ref[...] - step * PACKED == iota((PACKED, TOK), 0))
    rows = jnp.dot(chosen, feat_ref[...], preferred_element_type=F32).astype(BF16)
    for c in range(4):
        out_ref[:, c * CAP : (c + 1) * CAP, :] = rows[:, c * 128 : (c + 1) * 128].reshape(PACKED // CAP, CAP, 128)
    info = lax.dot_general(
        info_ref[...], chosen, (((1,), (1,)), ((), ())), preferred_element_type=F32
    )
    group = iota((8, 128), 1) // CAP
    for d in range(PACKED // CAP):
        own = jnp.where(group == d % 4, info[:8, d // 4 * 128 : d // 4 * 128 + 128], 0.0)
        own = own + pltpu.roll(own, 64, 1)
        own = own + pltpu.roll(own, 32, 1)
        out_ref[d, 4 * CAP :, :] = own.astype(BF16)


PACKED = 512


def pack(cells, features):
    return pl.pallas_call(
        pack_kernel,
        grid=(BANDS * CAP // PACKED,),
        in_specs=[
            pl.BlockSpec((1, TOK), lambda i: (0, 0)),
            pl.BlockSpec((TOK, LOCAL), lambda i: (0, 0)),
        ],
        out_specs=pl.BlockSpec((PACKED // CAP, MSG, 128), lambda i: (i, 0, 0)),
        out_shape=jax.ShapeDtypeStruct((BANDS, MSG, 128), BF16),
        scratch_shapes=[pltpu.VMEM((1, TOK), jnp.int32), pltpu.VMEM((16, TOK), BF16)],
        compiler_params=params(20),
        name="pack",
    )(cells.reshape(1, TOK), features)


def place_kernel(msg_ref, first_ref, last_ref, place_ref):
    step = pl.program_id(0)

    @pl.when(step == 0)
    def _():
        info = msg_ref[:, 4 * CAP :, :].astype(F32).reshape(16, 4, 8, 128)
        shape = (16, 4, 8, 128)
        info = jnp.sum(jnp.where(iota(shape, 3) // CAP == iota(shape, 1), info, 0.0), axis=1)
        place_ref[...] = (info[:, 0, :] * 32.0 + info[:, 1, :]).astype(jnp.int32) - 32

    cell = iota((256, 128), 0) + step * 256
    chosen = jnp.concatenate(
        [ones_where(place_ref[g : g + 1, :] == cell) for g in range(16)], axis=1
    )
    rows = jnp.concatenate(
        [msg_ref[:, c * CAP : (c + 1) * CAP, :].reshape(BANDS * CAP, 128) for c in range(4)],
        axis=1,
    )
    row = jnp.dot(chosen, rows, preferred_element_type=F32).astype(BF16)

    @pl.when(step < 3)
    def _():
        first_ref[...] = row

    @pl.when(step > 0)
    def _():
        last_ref[...] = row


def place(messages):
    return pl.pallas_call(
        place_kernel,
        grid=(4,),
        in_specs=[pl.BlockSpec((BANDS, MSG, 128), lambda i: (0, 0, 0))],
        out_specs=[
            pl.BlockSpec((256, LOCAL), lambda i: (jnp.minimum(i, 2), 0)),
            pl.BlockSpec((256, LOCAL), lambda i: (jnp.maximum(i - 1, 0), 0)),
        ],
        out_shape=[jax.ShapeDtypeStruct((768, LOCAL), BF16)] * 2,
        scratch_shapes=[pltpu.VMEM((16, 128), jnp.int32)],
        compiler_params=params(20),
        name="place",
    )(messages)


def spread_row(x_ref, r, rows):
    sub = iota((3, 8, 128), 1)
    x = rows.astype(F32).reshape(32, 8, 128)
    x_ref[r, 3:35] = x
    x_ref[r, 0:3] = jnp.where(sub == 0, 0.0, pltpu.roll(x[29:32], 1, 1))
    x_ref[r, 35:38] = jnp.where(sub == 7, 0.0, pltpu.roll(x[0:3], 7, 1))


def spread_taps(tap_ref, w_ref):
    for t in range(49):
        tap_ref[t] = jnp.broadcast_to(w_ref[t : t + 1, :], (8, 128))


def grid_row(ref, at):
    return ref[at * 256 : (at + 1) * 256, :]


def add_taps(acc, x_ref, tap_ref, k, inputs):
    for j in range(7):
        for r, uses in enumerate(inputs):
            taps = [(o, tap_ref[i * 7 + j]) for o, i in uses]
            for n in range(len(acc[0])):
                x = x_ref[r, k + j + n]
                for o, tap in taps:
                    acc[o][n] = acc[o][n] + x * tap


def conv_own_kernel(first_ref, last_ref, w_ref, bias_ref, out_ref, x_ref, tap_ref):
    for r in range(4):
        spread_row(x_ref, r, grid_row(first_ref, r) if r < 3 else grid_row(last_ref, 2))
    spread_taps(tap_ref, w_ref)
    bias = jnp.broadcast_to(bias_ref[...], (8, 128))
    inputs = [[(o, r - o + 3) for o in range(4)] for r in range(4)]

    def group(g, carry):
        k = g * 4
        acc = [[bias] * 4 for _ in range(4)]
        add_taps(acc, x_ref, tap_ref, k, inputs)
        for o in range(4):
            for n in range(4):
                out_ref[o * 32 + k + n] = acc[o][n]
        return carry

    lax.fori_loop(0, 8, group, 0)


def conv_own(first, last, taps, bias):
    column = lambda rows: pl.BlockSpec((rows, 128), lambda i: (0, i))
    return pl.pallas_call(
        conv_own_kernel,
        grid=(4,),
        in_specs=[column(768), column(768), column(49), column(1)],
        out_specs=pl.BlockSpec((128, 8, 128), lambda i: (0, 0, i)),
        out_shape=jax.ShapeDtypeStruct((128, 8, LOCAL), F32),
        scratch_shapes=[pltpu.VMEM((4, 38, 8, 128), F32), pltpu.VMEM((49, 8, 128), F32)],
        compiler_params=params(8),
        cost_estimate=pl.CostEstimate(
            flops=8 * TOK * TOK * LOCAL, bytes_accessed=4 * 2**20, transcendentals=0
        ),
        name="conv_own",
    )(first, last, taps, bias)


def conv_edge_kernel(part_ref, far_ref, near_ref, w_ref, out_ref, x_ref, tap_ref, nat_ref, *, upper):
    sources = [grid_row(far_ref, r) for r in range(3)] + [near_ref[...]]
    for r, rows in enumerate(sources):
        spread_row(x_ref, r, rows)
    spread_taps(tap_ref, w_ref)
    if upper:
        at = [-3, -2, -1, 4]
        outs = [0, 1]
    else:
        at = [4, 5, 6, -1]
        outs = [2, 3]
    inputs = [
        [(o, at[r] - out + 3) for o, out in enumerate(outs) if 0 <= at[r] - out + 3 < 7]
        for r in range(4)
    ]

    def group(g, carry):
        k = g * 8
        acc = [[part_ref[o * 32 + k + n] for n in range(8)] for o in range(2)]
        add_taps(acc, x_ref, tap_ref, k, inputs)
        for o in range(2):
            for n in range(8):
                nat_ref[pl.ds(o * 256 + k + n, 8, stride=32), :] = acc[o][n]
        return carry

    lax.fori_loop(0, 4, group, 0)
    out_ref[...] = nat_ref[...].astype(BF16)


def conv_edge(part, above, below, taps, upper):
    column = lambda rows, at=0: pl.BlockSpec((rows, 128), lambda i: (at, i))
    far, near = (above, below) if upper else (below, above)
    return pl.pallas_call(
        functools.partial(conv_edge_kernel, upper=upper),
        grid=(4,),
        in_specs=[
            pl.BlockSpec((64, 8, 128), lambda i: (0 if upper else 1, 0, i)),
            column(768),
            column(256, 0 if upper else 2),
            column(49),
        ],
        out_specs=column(512),
        out_shape=jax.ShapeDtypeStruct((512, LOCAL), BF16),
        scratch_shapes=[
            pltpu.VMEM((4, 38, 8, 128), F32),
            pltpu.VMEM((49, 8, 128), F32),
            pltpu.VMEM((512, 128), F32),
        ],
        compiler_params=params(8),
        cost_estimate=pl.CostEstimate(
            flops=2 * TOK * TOK * LOCAL, bytes_accessed=4 * 2**20, transcendentals=0
        ),
        name="conv_upper" if upper else "conv_lower",
    )(part, far, near, taps)


def project_kernel(half_ref, own_ref, other_ref, w_own_ref, w_other_ref, kv_ref, q_ref):
    step = pl.program_id(0)
    out = (
        jnp.dot(own_ref[...], w_own_ref[...], preferred_element_type=F32)
        + jnp.dot(other_ref[...], w_other_ref[...], preferred_element_type=F32)
    ).astype(BF16)

    @pl.when(step < 2)
    def _():
        kv_ref[...] = out

    @pl.when(step == 2)
    def _():
        q_ref[...] = out


def project(half, own, other, weights):
    rows = own.shape[0]
    third = lambda j: jnp.where(j == 2, 0, j + 1)
    return pl.pallas_call(
        project_kernel,
        grid_spec=pltpu.PrefetchScalarGridSpec(
            num_scalar_prefetch=1,
            grid=(3,),
            in_specs=[
                pl.BlockSpec((rows, LOCAL), lambda j, h: (0, 0)),
                pl.BlockSpec((rows, LOCAL), lambda j, h: (0, 0)),
                pl.BlockSpec((LOCAL, LOCAL), lambda j, h: (h[0], third(j))),
                pl.BlockSpec((LOCAL, LOCAL), lambda j, h: (1 - h[0], third(j))),
            ],
            out_specs=[
                pl.BlockSpec((rows, LOCAL), lambda j, h: (0, jnp.minimum(j, 1))),
                pl.BlockSpec((rows, LOCAL), lambda j, h: (0, 0)),
            ],
        ),
        out_shape=[
            jax.ShapeDtypeStruct((rows, 2 * LOCAL), BF16),
            jax.ShapeDtypeStruct((rows, LOCAL), BF16),
        ],
        compiler_params=params(12),
        cost_estimate=pl.CostEstimate(
            flops=2 * rows * D * 3 * LOCAL, bytes_accessed=6 * 2**20, transcendentals=0
        ),
        name="project",
    )(half, own, other, weights, weights)


KCHUNK = 256


def partial_attention(queries, keys, values, scores_ref):
    columns = jnp.transpose(values.astype(F32)).astype(BF16)
    ones = jnp.ones((16, keys.shape[0]), BF16)
    columns = [jnp.concatenate([columns[h * 64 : h * 64 + 64], ones], axis=0) for h in range(2)]
    lane = iota(queries[0].shape, 1)
    chunks = [slice(c, c + KCHUNK) for c in range(0, keys.shape[0], KCHUNK)]

    def query(step):
        mine = (lane // 64) == step % 2
        return jnp.where(mine, queries[step // 2] * 0.125, 0.0).astype(BF16)

    def scores(step, at, q, top):
        s = lax.dot_general(keys[at], q, (((1,), (1,)), ((), ())), preferred_element_type=F32)
        scores_ref[step % 2, at, :] = s
        high = jnp.max(s.reshape(KCHUNK // 8, 8, s.shape[1]), axis=0)
        return high if top is None else jnp.maximum(top, high)

    q, top = query(0), None
    for at in chunks:
        top = scores(0, at, q, top)
    steps = 2 * len(queries)
    for step in range(steps):
        top = jnp.max(top, axis=0, keepdims=True)
        q = query(step + 1) if step + 1 < steps else None
        summed = following = None
        for at in chunks:
            if q is not None:
                following = scores(step + 1, at, q, following)
            weight = jnp.exp(scores_ref[step % 2, at, :] - top).astype(BF16)
            part = jnp.dot(columns[step % 2][:, at], weight, preferred_element_type=F32)
            summed = part if summed is None else summed + part
        yield summed[:64], summed[64:65], top
        top = following


def blocks_of(size, *refs):
    return [ref[r : r + size, :] for ref in refs for r in range(0, ref.shape[0], size)]


def stacked(*refs):
    return jnp.concatenate([ref[...] for ref in refs], axis=0)


def attend_kernel(*refs, parts, resumed, final):
    queries, keys, values = refs[:2], refs[2 : 2 + parts], refs[2 + parts : 2 + 2 * parts]
    refs = refs[2 + 2 * parts :]
    if resumed:
        old_acc_ref, old_stat_ref, *refs = refs
    *outs, scores_ref = refs
    size = 512 // parts
    heads = []
    steps = partial_attention(blocks_of(size, *queries), stacked(*keys), stacked(*values), scores_ref)
    for step, (acc, total, top) in enumerate(steps):
        block, head = divmod(step, 2)
        at = slice(block * size, (block + 1) * size)
        rows = slice(head * 64, head * 64 + 64)
        if resumed:
            old_total = old_stat_ref[0, head : head + 1, at]
            old_top = old_stat_ref[0, head + 2 : head + 3, at]
            highest = jnp.maximum(top, old_top)
            here, there = jnp.exp(top - highest), jnp.exp(old_top - highest)
            total = total * here + old_total * there
            acc = acc * here + old_acc_ref[rows, at] * there
            top = highest
        if not final:
            outs[0][rows, at] = acc
            outs[1][0, head : head + 1, at] = total
            outs[1][0, head + 2 : head + 3, at] = top
            continue
        heads.append(acc / total)
        if head:
            outs[0][at, :] = jnp.transpose(jnp.concatenate(heads, axis=0)).astype(BF16)
            heads = []


def attend(queries, keys_values, state=(), final=False):
    column = lambda rows, first=0: pl.BlockSpec((rows, 128), lambda p: (0, first + p))
    parts = len(keys_values)
    count = 512 * parts
    states = [pl.BlockSpec((128, TOK), lambda p: (p, 0)), pl.BlockSpec((1, 8, TOK), lambda p: (p, 0, 0))]
    state_shapes = [
        jax.ShapeDtypeStruct((LOCAL, TOK), F32),
        jax.ShapeDtypeStruct((4, 8, TOK), F32),
    ]
    return pl.pallas_call(
        functools.partial(attend_kernel, parts=parts, resumed=bool(state), final=final),
        grid=(4,),
        in_specs=[column(512)] * (2 + parts) + [column(512, 4)] * parts + (states if state else []),
        out_specs=column(TOK) if final else states,
        out_shape=jax.ShapeDtypeStruct((TOK, LOCAL), BF16) if final else state_shapes,
        scratch_shapes=[pltpu.VMEM((2, count, 512 // parts), F32)],
        compiler_params=params(ATTENTION_VMEM),
        cost_estimate=pl.CostEstimate(
            flops=4 * TOK * count * LOCAL, bytes_accessed=6 * 2**20, transcendentals=8 * TOK * count
        ),
        name="last_keys" if final else ("more_keys" if state else "own_keys"),
    )(*queries, *keys_values, *keys_values, *state)


ATTENTION_VMEM = 24


def merged_taps(conv7, conv5, conv3):
    taps = conv7.astype(F32)
    taps = taps + jnp.pad(conv5.astype(F32), ((1, 1), (1, 1), (0, 0)))
    taps = taps + jnp.pad(conv3.astype(F32), ((2, 2), (2, 2), (0, 0)))
    return taps.reshape(49, LOCAL) + (jnp.arange(49) == 24).astype(F32)[:, None]


def shards(features, cells, conv7, conv5, conv3, conv_bias, w_qkv):
    messages = pack(cells, features)
    arrived = lax.all_to_all(messages, "seq", split_axis=0, concat_axis=0, tiled=True)
    first, last = place(arrived)
    up = [(i, i + 1) for i in range(BANDS - 1)]
    down = [(j, i) for i, j in up]
    above = lax.ppermute(last, "seq", up)
    below = lax.ppermute(first, "seq", down)
    taps = merged_taps(conv7, conv5, conv3)
    bias = conv_bias.astype(F32).reshape(1, LOCAL)
    weights = w_qkv.reshape(D, 3 * LOCAL)
    half = lax.axis_index("head").astype(jnp.int32).reshape(1)
    ring = [(i, (i + 1) % BANDS) for i in range(BANDS)]
    part = conv_own(first, last, taps, bias)
    mixed = [conv_edge(part, above, below, taps, upper) for upper in (False, True)]
    others = [lax.ppermute(own, "head", [(0, 1), (1, 0)]) for own in mixed]
    keys_values, queries = zip(
        *[project(half, own, other, weights) for own, other in zip(mixed, others)]
    )
    first_prior, last_prior = [lax.ppermute(block, "seq", ring) for block in keys_values]
    queries = queries[::-1]
    state = attend(queries, keys_values)
    state = attend(queries, [first_prior], state)
    return attend(queries, [last_prior], state, final=True)


def solution(mesh):
    placed = (
        P("seq", "head"),
        P("seq"),
        P(None, None, "head"),
        P(None, None, "head"),
        P(None, None, "head"),
        P("head"),
        P(None, None, "head"),
    )
    return jax.shard_map(
        shards, mesh=mesh, in_specs=placed, out_specs=P("seq", "head"), check_vma=False
    )
```

```python
import functools
import math

import jax
import jax.numpy as jnp
from jax import lax
from jax.experimental import pallas as pl
from jax.experimental.pallas import tpu as pltpu
from jax.sharding import PartitionSpec as P

D = 1024
HEADS = 16
GRID_W = 256
BANDS = 64
TOK = 1024
LOCAL = 512
CAP = 32
MSG = 4 * CAP + 8
BF16 = jnp.bfloat16
F32 = jnp.float32


def iota(shape, dim):
    return lax.broadcasted_iota(jnp.int32, shape, dim)


def ones_where(mask):
    return jnp.where(mask, 1.0, 0.0).astype(BF16)


def params(mebibytes):
    return pltpu.CompilerParams(vmem_limit_bytes=mebibytes * 2**20)


def pack_kernel(cells_ref, feat_ref, out_ref, slot_ref, info_ref):
    step = pl.program_id(0)

    @pl.when(step == 0)
    def _():
        cells = cells_ref[...]
        band = cells >> 10
        within = cells & (TOK - 1)
        member = jnp.where(iota((BANDS, TOK), 0) == band, 1.0, 0.0)
        before = ones_where(iota((TOK, TOK), 0) < iota((TOK, TOK), 1))
        counts = jnp.dot(member.astype(BF16), before, preferred_element_type=F32)
        rank = jnp.sum(member * counts, axis=0, keepdims=True).astype(jnp.int32)
        slot_ref[...] = band * CAP + rank
        place = (within & 768) | ((within & 31) << 3) | ((within >> 5) & 7)
        row = iota((16, TOK), 0)
        info = jnp.where(row == 0, (place >> 5) + 1, jnp.where(row == 1, place & 31, 0))
        info_ref[...] = info.astype(F32).astype(BF16)

    chosen = ones_where(slot_ref[...] - step * PACKED == iota((PACKED, TOK), 0))
    rows = jnp.dot(chosen, feat_ref[...], preferred_element_type=F32).astype(BF16)
    for c in range(4):
        out_ref[:, c * CAP : (c + 1) * CAP, :] = rows[:, c * 128 : (c + 1) * 128].reshape(PACKED // CAP, CAP, 128)
    info = lax.dot_general(
        info_ref[...], chosen, (((1,), (1,)), ((), ())), preferred_element_type=F32
    )
    group = iota((8, 128), 1) // CAP
    for d in range(PACKED // CAP):
        own = jnp.where(group == d % 4, info[:8, d // 4 * 128 : d // 4 * 128 + 128], 0.0)
        own = own + pltpu.roll(own, 64, 1)
        own = own + pltpu.roll(own, 32, 1)
        out_ref[d, 4 * CAP :, :] = own.astype(BF16)


PACKED = 512


def pack(cells, features):
    return pl.pallas_call(
        pack_kernel,
        grid=(BANDS * CAP // PACKED,),
        in_specs=[
            pl.BlockSpec((1, TOK), lambda i: (0, 0)),
            pl.BlockSpec((TOK, LOCAL), lambda i: (0, 0)),
        ],
        out_specs=pl.BlockSpec((PACKED // CAP, MSG, 128), lambda i: (i, 0, 0)),
        out_shape=jax.ShapeDtypeStruct((BANDS, MSG, 128), BF16),
        scratch_shapes=[pltpu.VMEM((1, TOK), jnp.int32), pltpu.VMEM((16, TOK), BF16)],
        compiler_params=params(20),
        name="pack",
    )(cells.reshape(1, TOK), features)


def place_kernel(msg_ref, first_ref, last_ref, place_ref):
    step = pl.program_id(0)

    @pl.when(step == 0)
    def _():
        info = msg_ref[:, 4 * CAP :, :].astype(F32).reshape(16, 4, 8, 128)
        shape = (16, 4, 8, 128)
        info = jnp.sum(jnp.where(iota(shape, 3) // CAP == iota(shape, 1), info, 0.0), axis=1)
        place_ref[...] = (info[:, 0, :] * 32.0 + info[:, 1, :]).astype(jnp.int32) - 32

    cell = iota((256, 128), 0) + step * 256
    chosen = jnp.concatenate(
        [ones_where(place_ref[g : g + 1, :] == cell) for g in range(16)], axis=1
    )
    rows = jnp.concatenate(
        [msg_ref[:, c * CAP : (c + 1) * CAP, :].reshape(BANDS * CAP, 128) for c in range(4)],
        axis=1,
    )
    row = jnp.dot(chosen, rows, preferred_element_type=F32).astype(BF16)

    @pl.when(step < 3)
    def _():
        first_ref[...] = row

    @pl.when(step > 0)
    def _():
        last_ref[...] = row


def place(messages):
    return pl.pallas_call(
        place_kernel,
        grid=(4,),
        in_specs=[pl.BlockSpec((BANDS, MSG, 128), lambda i: (0, 0, 0))],
        out_specs=[
            pl.BlockSpec((256, LOCAL), lambda i: (jnp.minimum(i, 2), 0)),
            pl.BlockSpec((256, LOCAL), lambda i: (jnp.maximum(i - 1, 0), 0)),
        ],
        out_shape=[jax.ShapeDtypeStruct((768, LOCAL), BF16)] * 2,
        scratch_shapes=[pltpu.VMEM((16, 128), jnp.int32)],
        compiler_params=params(20),
        name="place",
    )(messages)


def spread_row(x_ref, r, rows):
    sub = iota((3, 8, 128), 1)
    x = rows.astype(F32).reshape(32, 8, 128)
    x_ref[r, 3:35] = x
    x_ref[r, 0:3] = jnp.where(sub == 0, 0.0, pltpu.roll(x[29:32], 1, 1))
    x_ref[r, 35:38] = jnp.where(sub == 7, 0.0, pltpu.roll(x[0:3], 7, 1))


def spread_taps(tap_ref, w_ref):
    for t in range(49):
        tap_ref[t] = jnp.broadcast_to(w_ref[t : t + 1, :], (8, 128))


def grid_row(ref, at):
    return ref[at * 256 : (at + 1) * 256, :]


def add_taps(acc, x_ref, tap_ref, k, inputs):
    for j in range(7):
        for r, uses in enumerate(inputs):
            taps = [(o, tap_ref[i * 7 + j]) for o, i in uses]
            for n in range(len(acc[0])):
                x = x_ref[r, k + j + n]
                for o, tap in taps:
                    acc[o][n] = acc[o][n] + x * tap


def conv_own_kernel(first_ref, last_ref, w_ref, bias_ref, out_ref, x_ref, tap_ref):
    for r in range(4):
        spread_row(x_ref, r, grid_row(first_ref, r) if r < 3 else grid_row(last_ref, 2))
    spread_taps(tap_ref, w_ref)
    bias = jnp.broadcast_to(bias_ref[...], (8, 128))
    inputs = [[(o, r - o + 3) for o in range(4)] for r in range(4)]

    def group(g, carry):
        k = g * 4
        acc = [[bias] * 4 for _ in range(4)]
        add_taps(acc, x_ref, tap_ref, k, inputs)
        for o in range(4):
            for n in range(4):
                out_ref[o * 32 + k + n] = acc[o][n]
        return carry

    lax.fori_loop(0, 8, group, 0)


def conv_own(first, last, taps, bias):
    column = lambda rows: pl.BlockSpec((rows, 128), lambda i: (0, i))
    return pl.pallas_call(
        conv_own_kernel,
        grid=(4,),
        in_specs=[column(768), column(768), column(49), column(1)],
        out_specs=pl.BlockSpec((128, 8, 128), lambda i: (0, 0, i)),
        out_shape=jax.ShapeDtypeStruct((128, 8, LOCAL), F32),
        scratch_shapes=[pltpu.VMEM((4, 38, 8, 128), F32), pltpu.VMEM((49, 8, 128), F32)],
        compiler_params=params(8),
        cost_estimate=pl.CostEstimate(
            flops=8 * TOK * TOK * LOCAL, bytes_accessed=4 * 2**20, transcendentals=0
        ),
        name="conv_own",
    )(first, last, taps, bias)


def conv_edge_kernel(part_ref, far_ref, near_ref, w_ref, out_ref, x_ref, tap_ref, nat_ref, *, upper):
    sources = [grid_row(far_ref, r) for r in range(3)] + [near_ref[...]]
    for r, rows in enumerate(sources):
        spread_row(x_ref, r, rows)
    spread_taps(tap_ref, w_ref)
    if upper:
        at = [-3, -2, -1, 4]
        outs = [0, 1]
    else:
        at = [4, 5, 6, -1]
        outs = [2, 3]
    inputs = [
        [(o, at[r] - out + 3) for o, out in enumerate(outs) if 0 <= at[r] - out + 3 < 7]
        for r in range(4)
    ]

    def group(g, carry):
        k = g * 8
        acc = [[part_ref[o * 32 + k + n] for n in range(8)] for o in range(2)]
        add_taps(acc, x_ref, tap_ref, k, inputs)
        for o in range(2):
            for n in range(8):
                nat_ref[pl.ds(o * 256 + k + n, 8, stride=32), :] = acc[o][n]
        return carry

    lax.fori_loop(0, 4, group, 0)
    out_ref[...] = nat_ref[:512, :].astype(BF16)


def conv_edge(part, above, below, taps, upper):
    column = lambda rows, at=0: pl.BlockSpec((rows, 128), lambda i: (at, i))
    far, near = (above, below) if upper else (below, above)
    return pl.pallas_call(
        functools.partial(conv_edge_kernel, upper=upper),
        grid=(4,),
        in_specs=[
            pl.BlockSpec((64, 8, 128), lambda i: (0 if upper else 1, 0, i)),
            column(768),
            column(256, 0 if upper else 2),
            column(49),
        ],
        out_specs=column(512),
        out_shape=jax.ShapeDtypeStruct((512, LOCAL), BF16),
        scratch_shapes=[
            pltpu.VMEM((4, 38, 8, 128), F32),
            pltpu.VMEM((49, 8, 128), F32),
            pltpu.VMEM((512 + 32, 128), F32),
        ],
        compiler_params=params(8),
        cost_estimate=pl.CostEstimate(
            flops=2 * TOK * TOK * LOCAL, bytes_accessed=4 * 2**20, transcendentals=0
        ),
        name="conv_upper" if upper else "conv_lower",
    )(part, far, near, taps)


def project_kernel(half_ref, own_ref, other_ref, w_ref, kv_ref, q_ref, held_ref, sems):
    mine = pl.multiple_of(half_ref[0] * LOCAL, LOCAL)
    theirs = pl.multiple_of((1 - half_ref[0]) * LOCAL, LOCAL)
    copies = []
    for step, third in enumerate((1, 2, 0)):
        for side, start in enumerate((mine, theirs)):
            copies.append(
                pltpu.make_async_copy(
                    w_ref.at[third, pl.ds(start, LOCAL), :], held_ref.at[step, side], sems.at[step, side]
                )
            )
            copies[-1].start()
    own, other = own_ref[...], other_ref[...]
    for step in range(3):
        copies[2 * step].wait()
        copies[2 * step + 1].wait()
        out = (
            jnp.dot(own, held_ref[step, 0], preferred_element_type=F32)
            + jnp.dot(other, held_ref[step, 1], preferred_element_type=F32)
        ).astype(BF16)
        if step < 2:
            kv_ref[:, step * LOCAL : (step + 1) * LOCAL] = out
        else:
            q_ref[...] = out


def project(half, own, other, weights):
    rows = own.shape[0]
    return pl.pallas_call(
        project_kernel,
        in_specs=[
            pl.BlockSpec(memory_space=pltpu.SMEM),
            pl.BlockSpec((rows, LOCAL), lambda: (0, 0)),
            pl.BlockSpec((rows, LOCAL), lambda: (0, 0)),
            pl.BlockSpec(memory_space=pltpu.HBM),
        ],
        out_specs=[
            pl.BlockSpec((rows, 2 * LOCAL), lambda: (0, 0)),
            pl.BlockSpec((rows, LOCAL), lambda: (0, 0)),
        ],
        out_shape=[
            jax.ShapeDtypeStruct((rows, 2 * LOCAL), BF16),
            jax.ShapeDtypeStruct((rows, LOCAL), BF16),
        ],
        scratch_shapes=[
            pltpu.VMEM((3, 2, LOCAL, LOCAL), BF16),
            pltpu.SemaphoreType.DMA((3, 2)),
        ],
        compiler_params=params(16),
        cost_estimate=pl.CostEstimate(
            flops=2 * rows * D * 3 * LOCAL, bytes_accessed=6 * 2**20, transcendentals=0
        ),
        name="project",
    )(half, own, other, weights)


KCHUNK = 256


def partial_attention(queries, keys, values, scores_ref):
    columns = jnp.transpose(values.astype(F32)).astype(BF16)
    ones = jnp.ones((16, keys.shape[0]), BF16)
    columns = [jnp.concatenate([columns[h * 64 : h * 64 + 64], ones], axis=0) for h in range(2)]
    lane = iota(queries[0].shape, 1)
    chunks = [slice(c, c + KCHUNK) for c in range(0, keys.shape[0], KCHUNK)]

    def query(step):
        mine = (lane // 64) == step % 2
        return jnp.where(mine, queries[step // 2] * 0.125, 0.0).astype(BF16)

    def scores(step, at, q, top):
        s = lax.dot_general(keys[at], q, (((1,), (1,)), ((), ())), preferred_element_type=F32)
        scores_ref[step % 2, at, :] = s
        high = jnp.max(s.reshape(KCHUNK // 8, 8, s.shape[1]), axis=0)
        return high if top is None else jnp.maximum(top, high)

    q, top = query(0), None
    for at in chunks:
        top = scores(0, at, q, top)
    steps = 2 * len(queries)
    for step in range(steps):
        top = jnp.max(top, axis=0, keepdims=True)
        q = query(step + 1) if step + 1 < steps else None
        summed = following = None
        for at in chunks:
            if q is not None:
                following = scores(step + 1, at, q, following)
            weight = jnp.exp(scores_ref[step % 2, at, :] - top).astype(BF16)
            part = jnp.dot(columns[step % 2][:, at], weight, preferred_element_type=F32)
            summed = part if summed is None else summed + part
        yield summed[:64], summed[64:65], top
        top = following


def blocks_of(size, *refs):
    return [ref[r : r + size, :] for ref in refs for r in range(0, ref.shape[0], size)]


def stacked(*refs):
    return jnp.concatenate([ref[...] for ref in refs], axis=0)


def attend_kernel(*refs, parts, resumed, final):
    queries, keys, values = refs[:2], refs[2 : 2 + parts], refs[2 + parts : 2 + 2 * parts]
    refs = refs[2 + 2 * parts :]
    if resumed:
        old_acc_ref, old_stat_ref, *refs = refs
    *outs, scores_ref = refs
    size = 512 // parts
    heads = []
    steps = partial_attention(blocks_of(size, *queries), stacked(*keys), stacked(*values), scores_ref)
    for step, (acc, total, top) in enumerate(steps):
        block, head = divmod(step, 2)
        at = slice(block * size, (block + 1) * size)
        rows = slice(head * 64, head * 64 + 64)
        if resumed:
            old_total = old_stat_ref[0, head : head + 1, at]
            old_top = old_stat_ref[0, head + 2 : head + 3, at]
            highest = jnp.maximum(top, old_top)
            here, there = jnp.exp(top - highest), jnp.exp(old_top - highest)
            total = total * here + old_total * there
            acc = acc * here + old_acc_ref[rows, at] * there
            top = highest
        if not final:
            outs[0][rows, at] = acc
            outs[1][0, head : head + 1, at] = total
            outs[1][0, head + 2 : head + 3, at] = top
            continue
        heads.append(acc / total)
        if head:
            outs[0][at, :] = jnp.transpose(jnp.concatenate(heads, axis=0)).astype(BF16)
            heads = []


def attend(queries, keys_values, state=(), final=False):
    column = lambda rows, first=0: pl.BlockSpec((rows, 128), lambda p: (0, first + p))
    parts = len(keys_values)
    count = 512 * parts
    states = [pl.BlockSpec((128, TOK), lambda p: (p, 0)), pl.BlockSpec((1, 8, TOK), lambda p: (p, 0, 0))]
    state_shapes = [
        jax.ShapeDtypeStruct((LOCAL, TOK), F32),
        jax.ShapeDtypeStruct((4, 8, TOK), F32),
    ]
    return pl.pallas_call(
        functools.partial(attend_kernel, parts=parts, resumed=bool(state), final=final),
        grid=(4,),
        in_specs=[column(512)] * (2 + parts) + [column(512, 4)] * parts + (states if state else []),
        out_specs=column(TOK) if final else states,
        out_shape=jax.ShapeDtypeStruct((TOK, LOCAL), BF16) if final else state_shapes,
        scratch_shapes=[pltpu.VMEM((2, count, 512 // parts), F32)],
        compiler_params=params(ATTENTION_VMEM),
        cost_estimate=pl.CostEstimate(
            flops=4 * TOK * count * LOCAL, bytes_accessed=6 * 2**20, transcendentals=8 * TOK * count
        ),
        name="last_keys" if final else ("more_keys" if state else "own_keys"),
    )(*queries, *keys_values, *keys_values, *state)


ATTENTION_VMEM = 24


def merged_taps(conv7, conv5, conv3):
    taps = conv7.astype(F32)
    taps = taps + jnp.pad(conv5.astype(F32), ((1, 1), (1, 1), (0, 0)))
    taps = taps + jnp.pad(conv3.astype(F32), ((2, 2), (2, 2), (0, 0)))
    return taps.reshape(49, LOCAL) + (jnp.arange(49) == 24).astype(F32)[:, None]


def shards(features, cells, conv7, conv5, conv3, conv_bias, w_qkv):
    messages = pack(cells, features)
    arrived = lax.all_to_all(messages, "seq", split_axis=0, concat_axis=0, tiled=True)
    first, last = place(arrived)
    up = [(i, i + 1) for i in range(BANDS - 1)]
    down = [(j, i) for i, j in up]
    above = lax.ppermute(last, "seq", up)
    below = lax.ppermute(first, "seq", down)
    taps = merged_taps(conv7, conv5, conv3)
    bias = conv_bias.astype(F32).reshape(1, LOCAL)
    weights = jnp.transpose(w_qkv, (1, 0, 2))
    half = lax.axis_index("head").astype(jnp.int32).reshape(1)
    ring = [(i, (i + 1) % BANDS) for i in range(BANDS)]
    part = conv_own(first, last, taps, bias)
    mixed = [conv_edge(part, above, below, taps, upper) for upper in (False, True)]
    others = [lax.ppermute(own, "head", [(0, 1), (1, 0)]) for own in mixed]
    keys_values, queries = zip(
        *[project(half, own, other, weights) for own, other in zip(mixed, others)]
    )
    first_prior, last_prior = [lax.ppermute(block, "seq", ring) for block in keys_values]
    queries = queries[::-1]
    state = attend(queries, keys_values)
    state = attend(queries, [first_prior], state)
    return attend(queries, [last_prior], state, final=True)


def solution(mesh):
    placed = (
        P("seq", "head"),
        P("seq"),
        P(None, None, "head"),
        P(None, None, "head"),
        P(None, None, "head"),
        P("head"),
        P(None, None, "head"),
    )
    return jax.shard_map(
        shards, mesh=mesh, in_specs=placed, out_specs=P("seq", "head"), check_vma=False
    )
```
